256 devices in a mesh: seq: 16 (over z, core), head: 4 (over x), batch: 4 (over y).
Axes of the slice: x: 4, y: 4, z: 8, core: 2. Of those that a mesh axis runs over, the one named last changes fastest.
Arguments:
- queries: bfloat16 [4, 8192, 4096], P('batch', 'seq', 'head'), may hold values from -6 to 6
- key_rows: bfloat16 [4, 8192, 4096], P('batch', 'seq', 'head'), may hold values from -6 to 6
- value_rows: bfloat16 [4, 8192, 4096], P('batch', 'seq', 'head'), may hold values from -6 to 6
- head_gain: float32 [4096], P('head'), may hold values from 0.25 to 1.75
- in_proj: bfloat16 [4096, 1024], P('head'), may hold values from -0.09375 to 0.09375
- level_ids: int32 [4, 8192, 4], P('batch', 'seq'), may hold values from 0 to 2047
- level_table: bfloat16 [4, 2048, 1024], P(None, 'head'), may hold values from -6 to 6
- fine_gain: float32 [1024], replicated, may hold values from 0.25 to 1.75
- query_gain: float32 [64], replicated, may hold values from 0.5 to 3
- key_gain: float32 [64], replicated, may hold values from 0.5 to 3
- fine_qkv: bfloat16 [1024, 3072], P('seq'), may hold values from -0.1875 to 0.1875
- fine_out: bfloat16 [1024, 1024], P('seq'), may hold values from -0.1875 to 0.1875
Outputs:
- fine_hidden: bfloat16 [4, 8192, 4, 1024], P('batch', ('seq', 'head'))
The draws below stay inside these ranges and needn't reach their ends.
All inputs are finite; a program needn't handle non-finite values.
Results may differ from the reference program's by a relative error of at most 0.013.
Values may be sent and summed in bfloat16 or wider, within the bound.
A program may use at most 128 MiB of HBM per device.

```python
import math
import jax
import jax.numpy as jnp
from jax import lax

HEADS = 32
HD = 128
DF = 1024
FHEADS = 16
VOCAB = 2048
LEVELS = 4
TOK_DEV = 512
BATCH = 4
LENGTH = 8192
WIDTH = 4096
HEAD_DEV = 8
FHD = 64


def place_ends(result, own_key, smallest, high):
    shape = result.shape
    spot = [jax.random.randint(jax.random.fold_in(own_key, axis), (), 0, shape[axis]) for axis in range(len(shape))]
    result = result.at[tuple(spot)].set(smallest)
    longest = shape.index(max(shape))
    spot[longest] = (spot[longest] + 1) % shape[longest]
    return result.at[tuple(spot)].set(high)


def levels(stream_key, extent, cuts, least, top_value):
    def one(position, parts):
        heights = jax.random.uniform(jax.random.fold_in(jax.random.fold_in(stream_key, 6), position), (parts,), jnp.float32, least / len(cuts), top_value / len(cuts))
        return jnp.repeat(jnp.exp(heights), extent[position] // parts).reshape((-1,) + (1,) * (len(extent) - position - 1))

    gain = one(*cuts[0])
    for cut in cuts[1:]:
        gain = gain * one(*cut)
    return gain


def centred(rng, shape, width, limit, cuts=(), held_as=jnp.bfloat16):
    entries = jax.random.normal(rng, shape, jnp.float32) * width
    if len(cuts) > 0:
        entries = levels(rng, shape, cuts, -0.22, 0.18) * entries
    return jnp.clip(entries, min=-limit, max=limit).astype(held_as)


def setup_inputs(seed: int = 0) -> dict:
    key_of = jax.random.split(jax.random.key(seed), 13)
    return {
        "queries": centred(key_of[0], (BATCH, LENGTH, WIDTH), 1.0, 6.0, ((0, 4), (1, 16), (2, 4))),
        "key_rows": centred(key_of[1], (BATCH, LENGTH, WIDTH), 1.0, 6.0, ((0, 4), (1, 16), (2, 4))),
        "value_rows": centred(key_of[2], (BATCH, LENGTH, WIDTH), 1.0, 6.0, ((0, 4), (1, 16), (2, 4))),
        "head_gain": jnp.clip(1.0 + 0.15 * jax.random.normal(key_of[3], (WIDTH,), jnp.float32), 0.25, 1.75),
        "in_proj": centred(key_of[4], (WIDTH, DF), WIDTH ** -0.5, 0.09375, ((0, 4),)),
        "level_ids": place_ends(jax.random.randint(key_of[5], (BATCH, LENGTH, LEVELS), 0, VOCAB), jax.random.fold_in(key_of[5], 1), 0, VOCAB - 1).astype(jnp.int32),
        "level_table": centred(key_of[6], (LEVELS, VOCAB, DF), 1.0, 6.0, ((1, 4),)),
        "fine_gain": jnp.clip(1.0 + 0.15 * jax.random.normal(key_of[7], (DF,), jnp.float32), 0.25, 1.75),
        "query_gain": jnp.clip(jnp.exp(jax.random.uniform(key_of[8], (FHD,), jnp.float32, math.log(0.5), math.log(3.0))), 0.5, 3.0),
        "key_gain": jnp.clip(jnp.exp(jax.random.uniform(key_of[9], (FHD,), jnp.float32, math.log(0.5), math.log(3.0))), 0.5, 3.0),
        "fine_qkv": centred(key_of[10], (DF, 3 * DF), DF ** -0.5, 0.1875, ((0, 16),)),
        "fine_out": centred(key_of[11], (DF, DF), DF ** -0.5, 0.1875, ((0, 16),)),
    }


def rounded(value):
    return lax.optimization_barrier(value.astype(jnp.bfloat16)).astype(jnp.float32)

def coarse_sequence(queries, key_rows, value_rows, head_gain, in_proj):
    blocks = LENGTH // TOK_DEV
    query_blk = queries.reshape(blocks, TOK_DEV, HEADS, HD).astype(jnp.float32)
    key_blk = key_rows.reshape(blocks, TOK_DEV, HEADS, HD).astype(jnp.float32)
    value_blk = value_rows.reshape(blocks, TOK_DEV, HEADS, HD).astype(jnp.float32)
    states = jnp.einsum('cthd,cthe->chde', key_blk, value_blk, precision=lax.Precision.HIGHEST)
    running = jnp.cumsum(states, axis=0)
    carried = jnp.concatenate([jnp.zeros_like(states[:1]), running[:-1]], axis=0)
    causal = jnp.arange(TOK_DEV)[:, None] >= jnp.arange(TOK_DEV)[None, :]

    def one_block(pieces):
        query_one, key_one, value_one, carry_one = pieces
        scores = jnp.einsum('thd,shd->hts', query_one, key_one, precision=lax.Precision.HIGHEST)
        scores = rounded(jnp.where(causal[None], scores, jnp.zeros_like(scores)))
        local_part = jnp.einsum('hts,she->the', scores, value_one, precision=lax.Precision.HIGHEST)
        carried_part = jnp.einsum('thd,hde->the', query_one, carry_one, precision=lax.Precision.HIGHEST)
        return local_part + carried_part
    mixed = lax.map(one_block, (query_blk, key_blk, value_blk, carried))
    mixed = mixed.reshape(LENGTH, HEADS, HD)
    scale = lax.rsqrt(lax.optimization_barrier(jnp.mean(mixed * mixed, axis=-1, keepdims=True)) + 1e-06)
    normed = (mixed * scale).reshape(LENGTH, WIDTH) * head_gain
    normed = rounded(normed)
    groups = WIDTH // HEAD_DEV // HD
    grouped = normed.reshape(LENGTH, groups, HEAD_DEV * HD)
    weights = in_proj.astype(jnp.float32).reshape(groups, HEAD_DEV * HD, DF)
    partial_terms = jnp.einsum('tgc,gcd->tgd', grouped, weights, precision=lax.Precision.HIGHEST)
    return lax.optimization_barrier(jnp.sum(rounded(partial_terms), axis=1))

def fine_sequence(coarse_out, level_ids, level_table, fine_gain, query_gain, key_gain, fine_qkv, fine_out):
    looked = jnp.stack([jnp.take(level_table[which_level], level_ids[:, which_level], axis=0) for which_level in range(LEVELS)], axis=1)
    fine_in = coarse_out[:, None, :] + looked.astype(jnp.float32)
    flat = fine_in.reshape(LENGTH * LEVELS, DF)
    scale = lax.rsqrt(lax.optimization_barrier(jnp.mean(flat * flat, axis=-1, keepdims=True)) + 1e-05)
    fine_normed = (flat * scale * fine_gain).astype(jnp.bfloat16)
    projections = jnp.dot(fine_normed, fine_qkv, preferred_element_type=jnp.float32)
    shaped = projections.reshape(LENGTH, LEVELS, 3, FHEADS, FHD)
    query_part = shaped[:, :, 0]
    key_part = shaped[:, :, 1]
    value_part = shaped[:, :, 2]
    query_part = query_part * lax.rsqrt(lax.optimization_barrier(jnp.mean(query_part * query_part, axis=-1, keepdims=True)) + 1e-06) * query_gain
    key_part = key_part * lax.rsqrt(lax.optimization_barrier(jnp.mean(key_part * key_part, axis=-1, keepdims=True)) + 1e-06) * key_gain
    logits = jnp.einsum('flhd,fmhd->fhlm', query_part, key_part, precision=lax.Precision.HIGHEST) / math.sqrt(FHD)
    allowed = jnp.arange(LEVELS)[:, None] >= jnp.arange(LEVELS)[None, :]
    level_weights = jnp.where(allowed, jnp.exp(logits), jnp.zeros_like(logits))
    level_weights = level_weights / lax.optimization_barrier(jnp.sum(level_weights, axis=-1, keepdims=True))
    context = jnp.einsum('fhlm,fmhd->flhd', level_weights, value_part, precision=lax.Precision.HIGHEST)
    context = context.reshape(LENGTH * LEVELS, DF).astype(jnp.bfloat16)
    attended = jnp.dot(context, fine_out, preferred_element_type=jnp.float32)
    return (flat + attended).astype(jnp.bfloat16).reshape(LENGTH, LEVELS, DF)

def reference(queries, key_rows, value_rows, head_gain, in_proj, level_ids, level_table, fine_gain, query_gain, key_gain, fine_qkv, fine_out):

    def one_sequence(pieces):
        query_seq, key_seq, value_seq, ids_seq = pieces
        coarse_out = coarse_sequence(query_seq, key_seq, value_seq, head_gain, in_proj)
        return fine_sequence(coarse_out, ids_seq, level_table, fine_gain, query_gain, key_gain, fine_qkv, fine_out)
    return lax.map(one_sequence, (queries, key_rows, value_rows, level_ids))
```

```python
import functools
import math

import jax
import jax.numpy as jnp
from jax import lax
from jax.experimental import pallas as pl
from jax.experimental.pallas import tpu as pltpu
from jax.sharding import PartitionSpec as P

HD = 128
FHEADS = 16
CAP = 192
MESH = pl.DeviceIdType.MESH
F32 = jnp.float32
BF16 = jnp.bfloat16


def dot(a, b):
    return jnp.dot(a, b, preferred_element_type=F32)


def dot_rows(a, b):
    return lax.dot_general(a, b, (((0,), (0,)), ((), ())), preferred_element_type=F32)


def dot_cols(a, b):
    return lax.dot_general(a, b, (((1,), (1,)), ((), ())), preferred_element_type=F32)


def coarse_kernel(
    n_seq,
    n_head,
    n_bat,
    q_hbm,
    k_hbm,
    v_hbm,
    table_hbm,
    proj_hbm,
    ids_ref,
    gain_ref,
    coarse_ref,
    emb_ref,
    flag_ref,
    q_ref,
    k_ref,
    v_ref,
    table_ref,
    proj_ref,
    idb_ref,
    mixed_ref,
    state_out,
    state_in,
    carry_out,
    carry_in,
    rows_ref,
    rows_out,
    rows_in,
    part_out,
    part_in,
    flag_out,
    flag_in,
    load_sem,
    state_ssem,
    state_rsem,
    carry_ssem,
    carry_rsem,
    rows_ssem,
    rows_rsem,
    part_ssem,
    part_rsem,
    flag_ssem,
    flag_rsem,
):
    seq, head, bat = (lax.axis_index(a) for a in ("seq", "head", "batch"))
    tok, width = q_ref.shape
    heads = width // HD
    levels, vocab, df = table_ref.shape
    fr = tok // n_head
    piece = heads * HD // n_seq
    per_head = HD // piece

    loads = [
        pltpu.make_async_copy(src, dst, load_sem.at[i])
        for i, (src, dst) in enumerate(
            [(k_hbm, k_ref), (v_hbm, v_ref), (table_hbm, table_ref), (q_hbm, q_ref), (proj_hbm, proj_ref)]
        )
    ]
    for load in loads:
        load.start()

    barrier = pltpu.get_barrier_semaphore()

    def greet(axis, me, n):
        def one(t, c):
            pl.semaphore_signal(barrier, inc=1, device_id={axis: lax.rem(me + t, n)}, device_id_type=MESH)
            return c

        lax.fori_loop(1, n, one, 0)

    greet("seq", seq, n_seq)
    greet("head", head, n_head)
    greet("batch", bat, n_bat)

    for lv in range(levels):
        idb_ref[lv] = jnp.broadcast_to(ids_ref[:, lv : lv + 1], (tok, 128))

    lane = lax.broadcasted_iota(jnp.int32, (levels * fr, 128), 1)
    below = (
        lax.broadcasted_iota(jnp.int32, (levels * fr, levels * fr), 0)
        > lax.broadcasted_iota(jnp.int32, (levels * fr, levels * fr), 1)
    ).astype(BF16)

    def ids_of(dest):
        rows = pl.ds(pl.multiple_of(dest * fr, fr), fr)
        return jnp.concatenate([idb_ref[lv, rows, :] for lv in range(levels)], axis=0)

    def owned_by(dest, owner):
        ids = ids_of(dest)
        return jnp.where((ids >= owner * vocab) & (ids < (owner + 1) * vocab), 1.0, 0.0)

    def slots(dest, owner):
        mine = owned_by(dest, owner)
        rank = dot(below, mine.astype(BF16)).astype(jnp.int32)
        rank = jnp.where(mine > 0.5, rank, -1)
        wide = [(rank == lane + at).astype(F32).astype(BF16) for at in range(0, CAP, 128)]
        return jnp.concatenate(wide, axis=1)[:, :CAP]

    def most(d, worst):
        for t in range(1, n_head):
            worst = jnp.maximum(worst, jnp.sum(owned_by(d, lax.rem(d + t, n_head)), axis=0, keepdims=True))
        return worst

    worst = lax.fori_loop(0, n_head, most, jnp.zeros((1, 128), F32))
    over = jnp.where(worst > CAP, 1.0, 0.0)

    loads[0].wait()
    loads[1].wait()
    for h in range(heads):
        cols = slice(h * HD, (h + 1) * HD)
        state = dot_rows(k_ref[:, cols], v_ref[:, cols]).astype(BF16)
        for i in range(per_head):
            state_out[h * per_head + i, :piece] = state[i * piece : (i + 1) * piece]
    for p in range(n_seq):
        state_out[p, piece:] = jnp.broadcast_to(over, (16, 128)).astype(BF16)

    pl.semaphore_wait(barrier, n_seq + n_head + n_bat - 3)

    def state_copy(dest, src):
        return pltpu.make_async_remote_copy(
            src_ref=state_out.at[dest],
            dst_ref=state_in.at[src],
            send_sem=state_ssem.at[dest],
            recv_sem=state_rsem.at[src],
            device_id={"seq": dest},
            device_id_type=MESH,
        )

    def send_state(t, c):
        state_copy(lax.rem(seq + t, n_seq), seq).start()
        return c

    lax.fori_loop(1, n_seq, send_state, 0)
    state_in[seq] = state_out[seq]

    loads[2].wait()

    def look(dest, into):
        rows = pl.ds(pl.multiple_of(dest * fr, fr), fr)
        for lv in range(levels):
            ids = idb_ref[lv, rows, :] - head * vocab
            hot = jnp.concatenate(
                [(ids == lane[:fr] + at).astype(F32).astype(BF16) for at in range(0, vocab, 128)], axis=1
            )
            into[lv * fr : (lv + 1) * fr, :] = dot(hot, table_ref[lv]).astype(BF16)

    def rows_copy(t):
        return pltpu.make_async_remote_copy(
            src_ref=rows_out.at[t - 1],
            dst_ref=rows_in.at[t - 1],
            send_sem=rows_ssem.at[t - 1],
            recv_sem=rows_rsem.at[t - 1],
            device_id={"head": lax.rem(head + t, n_head)},
            device_id_type=MESH,
        )

    def send_rows(t, c):
        dest = lax.rem(head + t, n_head)
        look(dest, rows_ref)
        rows_out[t - 1] = dot_rows(slots(dest, head), rows_ref[...]).astype(BF16)
        rows_copy(t).start()
        return c

    lax.fori_loop(1, n_head, send_rows, 0)
    look(head, emb_ref)

    loads[3].wait()
    causal = lax.broadcasted_iota(jnp.int32, (fr, fr), 0) >= lax.broadcasted_iota(jnp.int32, (fr, fr), 1)

    def local_head(h, c):
        cols = pl.ds(pl.multiple_of(h * HD, HD), HD)
        for r in range(n_head):
            rows = slice(r * fr, (r + 1) * fr)
            qb = q_ref[rows, cols]
            diag = jnp.where(causal, dot_cols(qb, k_ref[rows, cols]), 0.0).astype(BF16)
            acc = dot(diag, v_ref[rows, cols])
            if r > 0:
                past = dot_cols(qb, k_ref[: r * fr, cols]).astype(BF16)
                acc = acc + dot(past, v_ref[: r * fr, cols])
            mixed_ref[rows, cols] = acc
        return c

    lax.fori_loop(0, heads, local_head, 0)

    def recv_state(t, c):
        src = lax.rem(seq + t, n_seq)
        state_copy(seq, src).wait_recv()
        return c

    lax.fori_loop(1, n_seq, recv_state, 0)
    run = jnp.zeros((piece, 128), F32)
    seen = jnp.zeros((16, 128), F32)
    for i in range(n_seq):
        carry_out[i] = run.astype(BF16)
        run = run + state_in[i, :piece].astype(F32)
        seen = jnp.maximum(seen, state_in[i, piece:].astype(F32))
    flag_out[...] = seen[:8]

    def carry_copy(dest, src):
        return pltpu.make_async_remote_copy(
            src_ref=carry_out.at[dest],
            dst_ref=carry_in.at[src],
            send_sem=carry_ssem.at[dest],
            recv_sem=carry_rsem.at[src],
            device_id={"seq": dest},
            device_id_type=MESH,
        )

    def send_carry(t, c):
        carry_copy(lax.rem(seq + t, n_seq), seq).start()
        return c

    lax.fori_loop(1, n_seq, send_carry, 0)
    carry_in[seq] = carry_out[seq]

    def flag_copy(t):
        return pltpu.make_async_remote_copy(
            src_ref=flag_out,
            dst_ref=flag_in.at[t - 1],
            send_sem=flag_ssem.at[t - 1],
            recv_sem=flag_rsem.at[t - 1],
            device_id={"batch": lax.rem(bat + t, n_bat)},
            device_id_type=MESH,
        )

    def send_flag(t, c):
        flag_copy(t).start()
        return c

    lax.fori_loop(1, n_bat, send_flag, 0)

    loads[4].wait()

    def recv_carry(t, c):
        src = lax.rem(seq + t, n_seq)
        carry_copy(seq, src).wait_recv()
        return c

    lax.fori_loop(1, n_seq, recv_carry, 0)

    def part_copy(t):
        return pltpu.make_async_remote_copy(
            src_ref=part_out.at[t - 1],
            dst_ref=part_in.at[t - 1],
            send_sem=part_ssem.at[t - 1],
            recv_sem=part_rsem.at[t - 1],
            device_id={"head": lax.rem(head + t, n_head)},
            device_id_type=MESH,
        )

    def project(dest):
        rows = pl.ds(pl.multiple_of(dest * fr, fr), fr)
        normed = []
        for h in range(heads):
            cols = slice(h * HD, (h + 1) * HD)
            carried = jnp.concatenate([carry_in[h * per_head + i] for i in range(per_head)], axis=0)
            mixed = mixed_ref[rows, cols] + dot(q_ref[rows, cols], carried)
            scale = lax.rsqrt(jnp.mean(mixed * mixed, axis=-1, keepdims=True) + 1e-06)
            normed.append((mixed * scale * gain_ref[:, cols]).astype(BF16))
        return dot(jnp.concatenate(normed, axis=1), proj_ref[...]).astype(BF16)

    def send_part(t, c):
        part_out[t - 1] = project(lax.rem(head + t, n_head))

        @pl.when(t < n_head)
        def _():
            part_copy(t).start()

        return c

    lax.fori_loop(1, n_head + 1, send_part, 0)

    def recv_rows(t, c):
        rows_copy(t).wait_recv()
        src = lax.rem(head + n_head - t, n_head)
        put = dot(slots(head, src), rows_in[t - 1])
        emb_ref[...] = (emb_ref[...].astype(F32) + put).astype(BF16)
        return c

    lax.fori_loop(1, n_head, recv_rows, 0)

    def recv_flag(t, seen):
        flag_copy(t).wait_recv()
        return jnp.maximum(seen, flag_in[t - 1])

    flag_ref[...] = lax.fori_loop(1, n_bat, recv_flag, seen[:8])

    coarse = part_out[n_head - 1].astype(F32)
    for t in range(1, n_head):
        part_copy(t).wait_recv()
        coarse = coarse + part_in[t - 1].astype(F32)
    coarse_ref[...] = coarse

    def sent(t, c):
        state_copy(lax.rem(seq + t, n_seq), seq).wait_send()
        carry_copy(lax.rem(seq + t, n_seq), seq).wait_send()
        return c

    lax.fori_loop(1, n_seq, sent, 0)
    for t in range(1, n_head):
        rows_copy(t).wait_send()
        part_copy(t).wait_send()
    for t in range(1, n_bat):
        flag_copy(t).wait_send()


def fine_kernel(
    coarse_ref, emb_ref, qkv_hbm, out_hbm, fgain_ref, qgain_ref, kgain_ref, o_ref, w_ref, wo_ref, n_ref, qkv_s, c_ref, sem
):
    fr, df = coarse_ref.shape
    rows = emb_ref.shape[0]
    levels = rows // fr
    fd = df // FHEADS
    wide = qkv_s.shape[2]
    tiles = df // wide
    loads = [
        pltpu.make_async_copy(qkv_hbm, w_ref, sem.at[0]),
        pltpu.make_async_copy(out_hbm, wo_ref, sem.at[1]),
    ]
    for load in loads:
        load.start()

    def norm(lv, c):
        at = pl.ds(pl.multiple_of(lv * fr, fr), fr)
        x = coarse_ref[...] + emb_ref[at, :].astype(F32)
        scale = lax.rsqrt(jnp.mean(x * x, axis=-1, keepdims=True) + 1e-05)
        n_ref[at, :] = (x * scale * fgain_ref[...]).astype(BF16)
        return c

    lax.fori_loop(0, levels, norm, 0)
    same = (
        lax.broadcasted_iota(jnp.int32, (wide, wide), 0) // fd == lax.broadcasted_iota(jnp.int32, (wide, wide), 1) // fd
    ).astype(F32).astype(BF16)

    def head_norm(x, gain):
        total = dot((x * x).astype(BF16), same)
        return x * lax.rsqrt(total * (1.0 / fd) + 1e-06) * gain

    loads[0].wait()
    step = 32

    def tile(j, c):
        at = pl.multiple_of(j * wide, wide)
        for part in range(3):
            y = dot(n_ref[...], w_ref[:, pl.ds(pl.multiple_of(part * df + j * wide, wide), wide)])
            if part == 0:
                y = head_norm(y, qgain_ref[...])
            elif part == 1:
                y = head_norm(y, kgain_ref[...])
            qkv_s[part] = y

        def frames(i, c):
            def get(part, lv):
                return qkv_s[part, pl.ds(pl.multiple_of(lv * fr + i * step, step), step), :]

            keys = [get(1, m) for m in range(levels)]
            vals = [get(2, m) for m in range(levels)]
            pairs = []
            for lv in range(1, levels):
                query = get(0, lv)
                pairs += [(query * keys[m]).astype(BF16) for m in range(lv + 1)]
            power = jnp.exp(dot(jnp.concatenate(pairs, axis=0), same))
            n = 0
            for lv in range(levels):
                if lv == 0:
                    ctx = vals[0]
                else:
                    es = [power[(n + m) * step : (n + m + 1) * step] for m in range(lv + 1)]
                    n += lv + 1
                    top = es[0] * vals[0]
                    bottom = es[0]
                    for m in range(1, lv + 1):
                        top = top + es[m] * vals[m]
                        bottom = bottom + es[m]
                    ctx = top / bottom
                c_ref[pl.ds(pl.multiple_of(lv * fr + i * step, step), step), pl.ds(at, wide)] = ctx.astype(BF16)
            return c

        lax.fori_loop(0, fr // step, frames, 0)
        return c

    lax.fori_loop(0, tiles, tile, 0)
    loads[1].wait()

    for lv in range(levels):
        at = slice(lv * fr, (lv + 1) * fr)

        def cols(j, c):
            to = pl.ds(pl.multiple_of(j * wide, wide), wide)
            x = coarse_ref[:, to] + emb_ref[at, to].astype(F32)
            y = x + dot(c_ref[at, :], wo_ref[:, to])
            o_ref[:, pl.ds(pl.multiple_of(lv * df + j * wide, wide), wide)] = y.astype(BF16)
            return c

        lax.fori_loop(0, tiles, cols, 0)


def missing_rows(level_ids, level_table, emb, n_head):
    levels, vocab, df = level_table.shape
    tok = level_ids.shape[0]
    fr = tok // n_head
    ids = level_ids.T.reshape(levels, n_head, fr).transpose(1, 0, 2).reshape(n_head, levels * fr)
    mine = ids - lax.axis_index("head") * vocab
    inside = (mine >= 0) & (mine < vocab)
    rank = jnp.cumsum(inside.astype(jnp.int32), axis=1) - 1
    dest = jnp.arange(n_head)[:, None]
    late = inside & (rank >= CAP) & (dest != lax.axis_index("head"))
    level = jnp.broadcast_to(jnp.arange(levels * fr)[None, :] // fr, mine.shape)
    rows = level_table[level, jnp.clip(mine, 0, vocab - 1)]
    rows = jnp.where(late[:, :, None], rows, jnp.zeros_like(rows))
    more = lax.psum_scatter(rows.reshape(n_head * levels * fr, df), "head", scatter_dimension=0, tiled=True)
    return (emb.astype(F32) + more.astype(F32)).astype(BF16)


def local(
    n_seq,
    n_head,
    n_bat,
    queries,
    key_rows,
    value_rows,
    head_gain,
    in_proj,
    level_ids,
    level_table,
    fine_gain,
    query_gain,
    key_gain,
    fine_qkv,
    fine_out,
):
    tok, width = queries.shape[1:]
    levels, vocab, df = level_table.shape
    heads = width // HD
    fr = tok // n_head
    rows = fr * levels
    piece = heads * HD // n_seq
    any_spec = pl.BlockSpec(memory_space=pl.ANY)
    vmem_spec = pl.BlockSpec(memory_space=pltpu.VMEM)
    dma = pltpu.SemaphoreType.DMA
    coarse, emb, flag = pl.pallas_call(
        functools.partial(coarse_kernel, n_seq, n_head, n_bat),
        out_shape=(
            jax.ShapeDtypeStruct((fr, df), F32),
            jax.ShapeDtypeStruct((rows, df), BF16),
            jax.ShapeDtypeStruct((8, 128), F32),
        ),
        in_specs=[any_spec] * 5 + [vmem_spec] * 2,
        out_specs=(vmem_spec,) * 3,
        scratch_shapes=[
            pltpu.VMEM((tok, width), BF16),
            pltpu.VMEM((tok, width), BF16),
            pltpu.VMEM((tok, width), BF16),
            pltpu.VMEM((levels, vocab, df), BF16),
            pltpu.VMEM((width, df), BF16),
            pltpu.VMEM((levels, tok, 128), jnp.int32),
            pltpu.VMEM((tok, width), F32),
            pltpu.VMEM((n_seq, piece + 16, 128), BF16),
            pltpu.VMEM((n_seq, piece + 16, 128), BF16),
            pltpu.VMEM((n_seq, piece, 128), BF16),
            pltpu.VMEM((n_seq, piece, 128), BF16),
            pltpu.VMEM((rows, df), BF16),
            pltpu.VMEM((n_head - 1, CAP, df), BF16),
            pltpu.VMEM((n_head - 1, CAP, df), BF16),
            pltpu.VMEM((n_head, fr, df), BF16),
            pltpu.VMEM((n_head - 1, fr, df), BF16),
            pltpu.VMEM((8, 128), F32),
            pltpu.VMEM((n_bat - 1, 8, 128), F32),
            dma((5,)),
            dma((n_seq,)),
            dma((n_seq,)),
            dma((n_seq,)),
            dma((n_seq,)),
            dma((n_head - 1,)),
            dma((n_head - 1,)),
            dma((n_head - 1,)),
            dma((n_head - 1,)),
            dma((n_bat - 1,)),
            dma((n_bat - 1,)),
        ],
        compiler_params=pltpu.CompilerParams(
            collective_id=0, has_side_effects=True, vmem_limit_bytes=60 * 1024 * 1024
        ),
        cost_estimate=pl.CostEstimate(flops=6_000_000_000, bytes_accessed=100_000_000, transcendentals=0),
    )(
        queries[0],
        key_rows[0],
        value_rows[0],
        level_table,
        in_proj,
        level_ids[0],
        head_gain.reshape(1, width),
    )
    emb = lax.cond(
        jnp.max(flag) > 0.5,
        lambda e: missing_rows(level_ids[0], level_table, e, n_head),
        lambda e: e,
        emb,
    )
    all_qkv = lax.all_gather(fine_qkv, "seq", axis=0, tiled=True)
    all_out = lax.all_gather(fine_out, "seq", axis=0, tiled=True)
    fd = df // FHEADS
    wide = 256
    result = pl.pallas_call(
        fine_kernel,
        out_shape=jax.ShapeDtypeStruct((fr, levels * df), BF16),
        in_specs=[vmem_spec] * 2 + [any_spec] * 2 + [vmem_spec] * 3,
        out_specs=vmem_spec,
        scratch_shapes=[
            pltpu.VMEM((df, 3 * df), BF16),
            pltpu.VMEM((df, df), BF16),
            pltpu.VMEM((rows, df), BF16),
            pltpu.VMEM((3, rows, wide), F32),
            pltpu.VMEM((rows, df), BF16),
            dma((2,)),
        ],
        compiler_params=pltpu.CompilerParams(vmem_limit_bytes=60 * 1024 * 1024),
    )(
        coarse,
        emb,
        all_qkv,
        all_out,
        fine_gain.reshape(1, df),
        jnp.tile(query_gain / math.sqrt(fd), wide // fd).reshape(1, wide),
        jnp.tile(key_gain, wide // fd).reshape(1, wide),
    )
    return result.reshape(1, fr, levels, df)


def solution(mesh):
    placed = (
        P("batch", "seq", "head"),
        P("batch", "seq", "head"),
        P("batch", "seq", "head"),
        P("head"),
        P("head", None),
        P("batch", "seq", None),
        P(None, "head", None),
        P(),
        P(),
        P(),
        P("seq", None),
        P("seq", None),
    )
    return jax.shard_map(
        functools.partial(local, mesh.shape["seq"], mesh.shape["head"], mesh.shape["batch"]),
        mesh=mesh,
        in_specs=placed,
        out_specs=P("batch", ("seq", "head"), None, None),
        check_vma=False,
    )
```

```python
import functools
import math

import jax
import jax.numpy as jnp
from jax import lax
from jax.experimental import pallas as pl
from jax.experimental.pallas import tpu as pltpu
from jax.sharding import PartitionSpec as P

HD = 128
FHEADS = 16
CAP = 192
WIDE = 256
STEP = 32
MESH = pl.DeviceIdType.MESH
F32 = jnp.float32
BF16 = jnp.bfloat16


def dot(a, b):
    return jnp.dot(a, b, preferred_element_type=F32)


def dot_rows(a, b):
    return lax.dot_general(a, b, (((0,), (0,)), ((), ())), preferred_element_type=F32)


def dot_cols(a, b):
    return lax.dot_general(a, b, (((1,), (1,)), ((), ())), preferred_element_type=F32)


def layer_kernel(
    cap,
    n_seq,
    n_head,
    n_bat,
    q_hbm,
    k_hbm,
    v_hbm,
    table_hbm,
    proj_hbm,
    qkv_hbm,
    out_hbm,
    ids_ref,
    gain_ref,
    fgain_ref,
    qgain_ref,
    kgain_ref,
    o_ref,
    flag_ref,
    coarse_ref,
    emb_ref,
    q_ref,
    k_ref,
    v_ref,
    table_ref,
    proj_ref,
    idb_ref,
    mixed_ref,
    state_out,
    state_in,
    carry_out,
    carry_in,
    rows_ref,
    rows_out,
    rows_in,
    part_out,
    part_in,
    flag_out,
    flag_in,
    load_sem,
    state_ssem,
    state_rsem,
    carry_ssem,
    carry_rsem,
    rows_ssem,
    rows_rsem,
    part_ssem,
    part_rsem,
    flag_ssem,
    flag_rsem,
    w_ref,
    wo_ref,
    n_ref,
    c_ref,
    qkv_s,
    w_ssem,
    w_rsem,
):
    seq, head, bat = (lax.axis_index(a) for a in ("seq", "head", "batch"))
    tok, width = q_ref.shape
    heads = width // HD
    levels, vocab, df = table_ref.shape
    fr = tok // n_head
    n_z = n_seq // 2
    z, core = seq // 2, lax.rem(seq, 2)
    piece = heads * HD // n_seq
    per_head = HD // piece

    loads = [
        pltpu.make_async_copy(src, dst, load_sem.at[i])
        for i, (src, dst) in enumerate(
            [(k_hbm, k_ref), (v_hbm, v_ref), (table_hbm, table_ref), (q_hbm, q_ref), (proj_hbm, proj_ref), (qkv_hbm, w_ref.at[z, core]), (out_hbm, wo_ref.at[z, core])]
        )
    ]
    for load in loads:
        load.start()

    barrier = pltpu.get_barrier_semaphore()

    def greet(axis, me, n):
        def one(t, c):
            pl.semaphore_signal(barrier, inc=1, device_id={axis: lax.rem(me + t, n)}, device_id_type=MESH)
            return c

        lax.fori_loop(1, n, one, 0)

    greet("seq", seq, n_seq)
    greet("head", head, n_head)
    greet("batch", bat, n_bat)

    for lv in range(levels):
        idb_ref[lv] = jnp.broadcast_to(ids_ref[:, lv : lv + 1], (tok, 128))

    lane = lax.broadcasted_iota(jnp.int32, (levels * fr, 128), 1)
    below = (
        lax.broadcasted_iota(jnp.int32, (levels * fr, levels * fr), 0)
        > lax.broadcasted_iota(jnp.int32, (levels * fr, levels * fr), 1)
    ).astype(BF16)

    def ids_of(dest):
        rows = pl.ds(pl.multiple_of(dest * fr, fr), fr)
        return jnp.concatenate([idb_ref[lv, rows, :] for lv in range(levels)], axis=0)

    def owned_by(dest, owner):
        ids = ids_of(dest)
        return jnp.where((ids >= owner * vocab) & (ids < (owner + 1) * vocab), 1.0, 0.0)

    def slots(dest, owner):
        mine = owned_by(dest, owner)
        rank = dot(below, mine.astype(BF16)).astype(jnp.int32)
        rank = jnp.where(mine > 0.5, rank, -1)
        wide = [(rank == lane + at).astype(F32).astype(BF16) for at in range(0, cap, 128)]
        return jnp.concatenate(wide, axis=1)[:, :cap]

    def most(d, worst):
        for t in range(1, n_head):
            worst = jnp.maximum(worst, jnp.sum(owned_by(d, lax.rem(d + t, n_head)), axis=0, keepdims=True))
        return worst

    worst = lax.fori_loop(0, n_head, most, jnp.zeros((1, 128), F32))
    over = jnp.where(worst > cap, 1.0, 0.0)

    mats = ((qkv_hbm, w_ref), (out_hbm, wo_ref))

    def turn(n):
        return lax.rem(n_z + (2 * lax.rem(n, 2) - 1) * ((n + 1) // 2), n_z)

    def quarter(m, b):
        wide = mats[m][1].shape[3] // n_bat
        return pl.ds(pl.multiple_of(lax.rem(b, n_bat) * wide, wide), wide)

    def weight_copy(m, kind, n, src, dst, device):
        return pltpu.make_async_remote_copy(
            src_ref=src,
            dst_ref=dst,
            send_sem=w_ssem.at[m, kind, n],
            recv_sem=w_rsem.at[m, kind, n],
            device_id=device,
            device_id_type=MESH,
        )

    def along_z(m, n):
        cols = quarter(m, bat)
        to = lax.rem(z + turn(n), n_z)
        return weight_copy(
            m, 0, n, mats[m][0].at[:, cols], mats[m][1].at[z, core, :, cols], {"seq": 2 * to + core}
        )

    def block(n):
        return lax.rem(z + n_z - turn(n), n_z)

    def arrived_z(m, n):
        cols = quarter(m, bat)
        here = mats[m][1].at[block(n), core, :, cols]
        weight_copy(m, 0, n, here, here, {"seq": seq}).wait_recv()

    def along_y(m, n, side):
        here = mats[m][1].at[block(n), core, :, quarter(m, bat)]
        return weight_copy(m, 1 + side, n, here, here, {"batch": lax.rem(bat + (1, n_bat - 1)[side], n_bat)})

    def came_y(m, n, side):
        here = mats[m][1].at[block(n), core, :, quarter(m, bat + (n_bat - 1, 1)[side])]
        return weight_copy(m, 1 + side, n, here, here, {"batch": bat})

    def pass_y(m, n, side):
        half = mats[m][1].shape[2] // 2
        here = mats[m][1].at[
            block(n), core, side * half : (side + 1) * half, quarter(m, bat + (n_bat - 1, 1)[side])
        ]
        return weight_copy(m, 3 + side, n, here, here, {"batch": lax.rem(bat + (1, n_bat - 1)[side], n_bat)})

    def passed_y(m, n, side):
        half = mats[m][1].shape[2] // 2
        here = mats[m][1].at[block(n), core, side * half : (side + 1) * half, quarter(m, bat + 2)]
        return weight_copy(m, 3 + side, n, here, here, {"batch": bat})

    def across(m, n):
        here = mats[m][1].at[block(n), core]
        return weight_copy(m, 5, n, here, here, {"seq": 2 * z + 1 - core})

    def over_blocks(first, last, act):
        def one(n, c):
            act(n)
            return c

        lax.fori_loop(first, last, one, 0)

    def send_z(m, first, last):
        over_blocks(first, last, lambda n: along_z(m, n).start())

    def send_y(m, first, last):
        def act(n):
            arrived_z(m, n)
            for side in range(2):
                along_y(m, n, side).start()

        over_blocks(first, last, act)

    def send_on(m, first, last):
        def act(n):
            for side in range(2):
                came_y(m, n, side).wait_recv()
                pass_y(m, n, side).start()

        over_blocks(first, last, act)

    def send_across(m, first, last):
        def act(n):
            for side in range(2):
                passed_y(m, n, side).wait_recv()
            across(m, n).start()

        over_blocks(first, last, act)

    def got_across(m):
        def act(n):
            here = mats[m][1].at[block(n), 1 - core]
            weight_copy(m, 5, n, here, here, {"seq": seq}).wait_recv()

        over_blocks(0, n_z, act)

    def all_sent(m):
        def act(n):
            along_z(m, n).wait_send()
            for side in range(2):
                along_y(m, n, side).wait_send()
                pass_y(m, n, side).wait_send()
            across(m, n).wait_send()

        across(m, 0).wait_send()
        over_blocks(1, n_z, act)

    pl.semaphore_wait(barrier, n_seq + n_head + n_bat - 3)
    send_z(0, 1, 3)

    loads[0].wait()
    loads[1].wait()
    for h in range(heads):
        cols = slice(h * HD, (h + 1) * HD)
        state = dot_rows(k_ref[:, cols], v_ref[:, cols]).astype(BF16)
        for i in range(per_head):
            state_out[h * per_head + i, :piece] = state[i * piece : (i + 1) * piece]
    for p in range(n_seq):
        state_out[p, piece:] = jnp.broadcast_to(over, (16, 128)).astype(BF16)

    def state_copy(dest, src):
        return pltpu.make_async_remote_copy(
            src_ref=state_out.at[dest],
            dst_ref=state_in.at[src],
            send_sem=state_ssem.at[dest],
            recv_sem=state_rsem.at[src],
            device_id={"seq": dest},
            device_id_type=MESH,
        )

    def send_state(t, c):
        state_copy(lax.rem(seq + t, n_seq), seq).start()
        return c

    lax.fori_loop(1, n_seq, send_state, 0)
    state_in[seq] = state_out[seq]
    send_z(0, 3, 5)
    loads[5].wait()
    across(0, 0).start()

    loads[2].wait()

    def look(dest, into):
        rows = pl.ds(pl.multiple_of(dest * fr, fr), fr)
        for lv in range(levels):
            ids = idb_ref[lv, rows, :] - head * vocab
            hot = jnp.concatenate(
                [(ids == lane[:fr] + at).astype(F32).astype(BF16) for at in range(0, vocab, 128)], axis=1
            )
            into[lv * fr : (lv + 1) * fr, :] = dot(hot, table_ref[lv]).astype(BF16)

    def rows_copy(t):
        return pltpu.make_async_remote_copy(
            src_ref=rows_out.at[t - 1],
            dst_ref=rows_in.at[t - 1],
            send_sem=rows_ssem.at[t - 1],
            recv_sem=rows_rsem.at[t - 1],
            device_id={"head": lax.rem(head + t, n_head)},
            device_id_type=MESH,
        )

    def send_rows(t, c):
        dest = lax.rem(head + t, n_head)
        look(dest, rows_ref)
        rows_out[t - 1] = dot_rows(slots(dest, head), rows_ref[...]).astype(BF16)
        rows_copy(t).start()
        return c

    lax.fori_loop(1, n_head, send_rows, 0)
    send_y(0, 1, 3)
    look(head, emb_ref)

    loads[3].wait()
    causal = lax.broadcasted_iota(jnp.int32, (fr, fr), 0) >= lax.broadcasted_iota(jnp.int32, (fr, fr), 1)

    def local_head(h, c):
        cols = pl.ds(pl.multiple_of(h * HD, HD), HD)
        for r in range(n_head):
            rows = slice(r * fr, (r + 1) * fr)
            qb = q_ref[rows, cols]
            diag = jnp.where(causal, dot_cols(qb, k_ref[rows, cols]), 0.0).astype(BF16)
            acc = dot(diag, v_ref[rows, cols])
            if r > 0:
                past = dot_cols(qb, k_ref[: r * fr, cols]).astype(BF16)
                acc = acc + dot(past, v_ref[: r * fr, cols])
            mixed_ref[rows, cols] = acc
        return c

    lax.fori_loop(0, heads, local_head, 0)

    def recv_state(t, c):
        src = lax.rem(seq + t, n_seq)
        state_copy(seq, src).wait_recv()
        return c

    lax.fori_loop(1, n_seq, recv_state, 0)
    run = jnp.zeros((piece, 128), F32)
    seen = jnp.zeros((16, 128), F32)
    for i in range(n_seq):
        carry_out[i] = run.astype(BF16)
        run = run + state_in[i, :piece].astype(F32)
        seen = jnp.maximum(seen, state_in[i, piece:].astype(F32))
    flag_out[...] = seen[:8]

    def carry_copy(dest, src):
        return pltpu.make_async_remote_copy(
            src_ref=carry_out.at[dest],
            dst_ref=carry_in.at[src],
            send_sem=carry_ssem.at[dest],
            recv_sem=carry_rsem.at[src],
            device_id={"seq": dest},
            device_id_type=MESH,
        )

    def send_carry(t, c):
        carry_copy(lax.rem(seq + t, n_seq), seq).start()
        return c

    lax.fori_loop(1, n_seq, send_carry, 0)
    carry_in[seq] = carry_out[seq]
    send_z(0, 5, n_z)
    send_z(1, 1, n_z)
    loads[6].wait()
    across(1, 0).start()

    def flag_copy(t):
        return pltpu.make_async_remote_copy(
            src_ref=flag_out,
            dst_ref=flag_in.at[t - 1],
            send_sem=flag_ssem.at[t - 1],
            recv_sem=flag_rsem.at[t - 1],
            device_id={"batch": lax.rem(bat + t, n_bat)},
            device_id_type=MESH,
        )

    def send_flag(t, c):
        flag_copy(t).start()
        return c

    lax.fori_loop(1, n_bat, send_flag, 0)
    send_on(0, 1, 3)
    send_y(0, 3, 5)
    loads[4].wait()

    def recv_carry(t, c):
        src = lax.rem(seq + t, n_seq)
        carry_copy(seq, src).wait_recv()
        return c

    lax.fori_loop(1, n_seq, recv_carry, 0)

    def part_copy(t):
        return pltpu.make_async_remote_copy(
            src_ref=part_out.at[t - 1],
            dst_ref=part_in.at[t - 1],
            send_sem=part_ssem.at[t - 1],
            recv_sem=part_rsem.at[t - 1],
            device_id={"head": lax.rem(head + t, n_head)},
            device_id_type=MESH,
        )

    def project(dest):
        rows = pl.ds(pl.multiple_of(dest * fr, fr), fr)
        normed = []
        for h in range(heads):
            cols = slice(h * HD, (h + 1) * HD)
            carried = jnp.concatenate([carry_in[h * per_head + i] for i in range(per_head)], axis=0)
            mixed = mixed_ref[rows, cols] + dot(q_ref[rows, cols], carried)
            scale = lax.rsqrt(jnp.mean(mixed * mixed, axis=-1, keepdims=True) + 1e-06)
            normed.append((mixed * scale * gain_ref[:, cols]).astype(BF16))
        return dot(jnp.concatenate(normed, axis=1), proj_ref[...]).astype(BF16)

    def send_part(t, c):
        part_out[t - 1] = project(lax.rem(head + t, n_head))

        @pl.when(t < n_head)
        def _():
            part_copy(t).start()

        return c

    lax.fori_loop(1, n_head + 1, send_part, 0)

    send_on(0, 3, 5)
    send_y(0, 5, n_z)
    send_across(0, 1, 5)

    def recv_rows(t, c):
        rows_copy(t).wait_recv()
        src = lax.rem(head + n_head - t, n_head)
        put = dot(slots(head, src), rows_in[t - 1])
        emb_ref[...] = (emb_ref[...].astype(F32) + put).astype(BF16)
        return c

    lax.fori_loop(1, n_head, recv_rows, 0)
    send_on(0, 5, n_z)
    send_y(1, 1, n_z)
    send_across(0, 5, n_z)

    def recv_flag(t, seen):
        flag_copy(t).wait_recv()
        return jnp.maximum(seen, flag_in[t - 1])

    flag_ref[...] = lax.fori_loop(1, n_bat, recv_flag, seen[:8])

    coarse = part_out[n_head - 1].astype(F32)
    for t in range(1, n_head):
        part_copy(t).wait_recv()
        coarse = coarse + part_in[t - 1].astype(F32)
    coarse_ref[...] = coarse

    fd = df // FHEADS

    def norm(lv, c):
        at = pl.ds(pl.multiple_of(lv * fr, fr), fr)
        x = coarse_ref[...] + emb_ref[at, :].astype(F32)
        scale = lax.rsqrt(jnp.mean(x * x, axis=-1, keepdims=True) + 1e-05)
        n_ref[at, :] = (x * scale * fgain_ref[...]).astype(BF16)
        return c

    lax.fori_loop(0, levels, norm, 0)
    same = (
        (
            lax.broadcasted_iota(jnp.int32, (WIDE, WIDE), 0) // fd
            == lax.broadcasted_iota(jnp.int32, (WIDE, WIDE), 1) // fd
        )
        .astype(F32)
        .astype(BF16)
    )

    def head_norm(x, gain):
        total = dot((x * x).astype(BF16), same)
        return x * lax.rsqrt(total * (1.0 / fd) + 1e-06) * gain

    got_across(0)
    send_on(1, 1, n_z)

    def tile(j, c):
        at = pl.multiple_of(j * WIDE, WIDE)
        for part in range(3):
            cols = pl.ds(pl.multiple_of(part * df + j * WIDE, WIDE), WIDE)
            y = dot(n_ref[...], w_ref[:, :, :, cols].reshape(df, WIDE))
            if part == 0:
                y = head_norm(y, qgain_ref[...])
            elif part == 1:
                y = head_norm(y, kgain_ref[...])
            qkv_s[part] = y

        def frames(i, c):
            def get(part, lv):
                return qkv_s[part, pl.ds(pl.multiple_of(lv * fr + i * STEP, STEP), STEP), :]

            keys = [get(1, m) for m in range(levels)]
            vals = [get(2, m) for m in range(levels)]
            pairs = []
            for lv in range(1, levels):
                query = get(0, lv)
                pairs += [(query * keys[m]).astype(BF16) for m in range(lv + 1)]
            power = jnp.exp(dot(jnp.concatenate(pairs, axis=0), same))
            n = 0
            for lv in range(levels):
                if lv == 0:
                    ctx = vals[0]
                else:
                    es = [power[(n + m) * STEP : (n + m + 1) * STEP] for m in range(lv + 1)]
                    n += lv + 1
                    top = es[0] * vals[0]
                    bottom = es[0]
                    for m in range(1, lv + 1):
                        top = top + es[m] * vals[m]
                        bottom = bottom + es[m]
                    ctx = top / bottom
                c_ref[pl.ds(pl.multiple_of(lv * fr + i * STEP, STEP), STEP), pl.ds(at, WIDE)] = ctx.astype(BF16)
            return c

        lax.fori_loop(0, fr // STEP, frames, 0)

        @pl.when(j == 0)
        def _():
            send_across(1, 1, n_z)

        return c

    lax.fori_loop(0, df // WIDE, tile, 0)
    got_across(1)

    for lv in range(levels):
        at = slice(lv * fr, (lv + 1) * fr)

        def cols(j, c):
            to = pl.ds(pl.multiple_of(j * WIDE, WIDE), WIDE)
            x = coarse_ref[:, to] + emb_ref[at, to].astype(F32)
            y = x + dot(c_ref[at, :], wo_ref[:, :, :, to].reshape(df, WIDE))
            o_ref[:, pl.ds(pl.multiple_of(lv * df + j * WIDE, WIDE), WIDE)] = y.astype(BF16)
            return c

        lax.fori_loop(0, df // WIDE, cols, 0)

    all_sent(0)
    all_sent(1)

    def sent(t, c):
        state_copy(lax.rem(seq + t, n_seq), seq).wait_send()
        carry_copy(lax.rem(seq + t, n_seq), seq).wait_send()
        return c

    lax.fori_loop(1, n_seq, sent, 0)
    for t in range(1, n_head):
        rows_copy(t).wait_send()
        part_copy(t).wait_send()
    for t in range(1, n_bat):
        flag_copy(t).wait_send()


def local(
    n_seq,
    n_head,
    n_bat,
    queries,
    key_rows,
    value_rows,
    head_gain,
    in_proj,
    level_ids,
    level_table,
    fine_gain,
    query_gain,
    key_gain,
    fine_qkv,
    fine_out,
):
    tok, width = queries.shape[1:]
    levels, vocab, df = level_table.shape
    heads = width // HD
    fr = tok // n_head
    rows = fr * levels
    piece = heads * HD // n_seq
    any_spec = pl.BlockSpec(memory_space=pl.ANY)
    vmem_spec = pl.BlockSpec(memory_space=pltpu.VMEM)
    dma = pltpu.SemaphoreType.DMA
    fd = df // FHEADS
    args = (
        queries[0],
        key_rows[0],
        value_rows[0],
        level_table,
        in_proj,
        fine_qkv,
        fine_out,
        level_ids[0],
        head_gain.reshape(1, width),
        fine_gain.reshape(1, df),
        jnp.tile(query_gain / math.sqrt(fd), WIDE // fd).reshape(1, WIDE),
        jnp.tile(key_gain, WIDE // fd).reshape(1, WIDE),
    )

    def run(cap, collective_id):
        return pl.pallas_call(
            functools.partial(layer_kernel, cap, n_seq, n_head, n_bat),
            out_shape=(
                jax.ShapeDtypeStruct((fr, levels * df), BF16),
                jax.ShapeDtypeStruct((8, 128), F32),
            ),
            in_specs=[any_spec] * 7 + [vmem_spec] * 5,
            out_specs=(vmem_spec,) * 2,
            scratch_shapes=[
                pltpu.VMEM((fr, df), F32),
                pltpu.VMEM((rows, df), BF16),
                pltpu.VMEM((tok, width), BF16),
                pltpu.VMEM((tok, width), BF16),
                pltpu.VMEM((tok, width), BF16),
                pltpu.VMEM((levels, vocab, df), BF16),
                pltpu.VMEM((width, df), BF16),
                pltpu.VMEM((levels, tok, 128), jnp.int32),
                pltpu.VMEM((tok, width), F32),
                pltpu.VMEM((n_seq, piece + 16, 128), BF16),
                pltpu.VMEM((n_seq, piece + 16, 128), BF16),
                pltpu.VMEM((n_seq, piece, 128), BF16),
                pltpu.VMEM((n_seq, piece, 128), BF16),
                pltpu.VMEM((rows, df), BF16),
                pltpu.VMEM((n_head - 1, cap, df), BF16),
                pltpu.VMEM((n_head - 1, cap, df), BF16),
                pltpu.VMEM((n_head, fr, df), BF16),
                pltpu.VMEM((n_head - 1, fr, df), BF16),
                pltpu.VMEM((8, 128), F32),
                pltpu.VMEM((n_bat - 1, 8, 128), F32),
                dma((7,)),
                dma((n_seq,)),
                dma((n_seq,)),
                dma((n_seq,)),
                dma((n_seq,)),
                dma((n_head - 1,)),
                dma((n_head - 1,)),
                dma((n_head - 1,)),
                dma((n_head - 1,)),
                dma((n_bat - 1,)),
                dma((n_bat - 1,)),
                pltpu.VMEM((n_seq // 2, 2, df // n_seq, 3 * df), BF16),
                pltpu.VMEM((n_seq // 2, 2, df // n_seq, df), BF16),
                pltpu.VMEM((rows, df), BF16),
                pltpu.VMEM((rows, df), BF16),
                pltpu.VMEM((3, rows, WIDE), F32),
                dma((2, 6, n_seq // 2)),
                dma((2, 6, n_seq // 2)),
            ],
            compiler_params=pltpu.CompilerParams(
                collective_id=collective_id, has_side_effects=True, vmem_limit_bytes=60 * 1024 * 1024
            ),
        )(*args)

    result, over = run(CAP, 0)
    result = lax.cond(over[0, 0] > 0.5, lambda r: run(rows, 1)[0], lambda r: r, result)
    return result.reshape(1, fr, levels, df)


def solution(mesh):
    placed = (
        P("batch", "seq", "head"),
        P("batch", "seq", "head"),
        P("batch", "seq", "head"),
        P("head"),
        P("head", None),
        P("batch", "seq", None),
        P(None, "head", None),
        P(),
        P(),
        P(),
        P("seq", None),
        P("seq", None),
    )
    return jax.shard_map(
        functools.partial(local, mesh.shape["seq"], mesh.shape["head"], mesh.shape["batch"]),
        mesh=mesh,
        in_specs=placed,
        out_specs=P("batch", ("seq", "head"), None, None),
        check_vma=False,
    )
```
